32 devices in a mesh: group: 16 (over z, x, core), head: 2 (over y).
Axes of the slice: x: 2, y: 2, z: 4, core: 2. Of those that a mesh axis runs over, the one named last changes fastest.
Arguments:
- query: bfloat16 [16, 512, 5120], P('group', None, 'head'), may hold values from -1.7265625 to 1.7265625
- key: bfloat16 [16, 512, 5120], P('group', None, 'head'), may hold values from -1.7265625 to 1.7265625
- value: bfloat16 [16, 512, 5120], P('group', None, 'head'), may hold values from -6 to 6
- output: bfloat16 [16, 512, 5120], P('group', None, 'head'), may hold values from -1.5 to 1.5
- grad_out: bfloat16 [16, 512, 5120], P('group', 'head'), may hold values from -169 to 169
- log_sum: float32 [16, 40, 512], P('group', 'head'), as said below
- group_length: int32 [16], replicated, may hold values from 256 to 512, as said below
- cache_source: int32 [16], replicated, may hold values from -1 to 14, as said below
Outputs:
- grad_query: bfloat16 [16, 512, 5120], P('group', 'head')
- grad_key: bfloat16 [16, 512, 5120], P('group', 'head')
- grad_value: bfloat16 [16, 512, 5120], P('group', 'head')
The draws below stay inside these ranges and needn't reach their ends.
Inputs may be any that keep to these rules, and one draw needn't show every extreme that they name: group_length[c] counts the first, live token slots of group c; some group is full. cache_source[c] is c - 1 where group c attends the preceding group's cache and -1 where a rollout starts; it is -1 for group 0 and c - 1 for the last group. `log_sum`: each entry lies between ln(512) + 0.2 and ln(1024) + 0.8.
All inputs are finite; a program needn't handle non-finite values.
Results may differ from the reference program's by a relative error of at most 0.0049.
Values may be sent and summed in bfloat16 or wider, within the bound.
No kernel may reach another device: no remote copies, remote signals or barrier semaphores. Data moves between devices by JAX's collectives and lax.ppermute only.
A program may use at most 128 MiB of HBM per device.

```python
import math
import jax
import jax.numpy as jnp
from jax import lax

HEADS = 40
HEAD_DIM = 128
LEN = 512
GROUPS = 16


def draw_group_length(key, part):
    lengths = jax.random.randint(jax.random.fold_in(key, 11), (GROUPS,), LEN // 2, LEN + 1)
    full_at = jax.random.randint(jax.random.fold_in(key, 12), (), 0, GROUPS)
    return jnp.where(jnp.arange(GROUPS) == full_at, LEN, lengths).astype(jnp.int32)


def draw_cache_source(key, part):
    group_ids = jnp.arange(GROUPS, dtype=jnp.int32)
    linked = jax.random.randint(jax.random.fold_in(key, 21), (GROUPS,), 0, 4) > 0
    linked = linked & (group_ids > 0) | (group_ids == GROUPS - 1)
    return jnp.where(linked, group_ids - 1, -1).astype(jnp.int32)


def draw_log_sum(key, part):
    lower = math.log(LEN) + 0.2
    upper = math.log(2 * LEN) + 0.8
    unit = jax.random.uniform(jax.random.fold_in(key, 31), (GROUPS, HEADS, LEN), jnp.float32)
    return (lower + (upper - lower) * unit).astype(jnp.float32)


def block_levels(stream_key, dims, cuts, least, high):
    def one(axis_at, shards_of):
        steps = jax.random.uniform(jax.random.fold_in(jax.random.fold_in(stream_key, 6), axis_at), (shards_of,), jnp.float32, least / len(cuts), high / len(cuts))
        return jnp.repeat(jnp.exp(steps), dims[axis_at] // shards_of).reshape((-1,) + (1,) * (len(dims) - axis_at - 1))

    gain = one(*cuts[0])
    for cut in cuts[1:]:
        gain = gain * one(*cut)
    return gain


def centred(stream_key, dims, width, bound, shards=(), kind=jnp.bfloat16):
    gain = block_levels(stream_key, dims, shards, -0.22, 0.18) if shards else 1.0
    result = jax.random.normal(stream_key, dims, jnp.float32) * width * gain
    return jnp.minimum(jnp.maximum(result, -bound), bound).astype(kind)


def setup_inputs(seed: int = 0) -> dict:
    streams_of = jax.random.split(jax.random.key(seed), 9)
    return {
        "query": jnp.clip(jax.random.uniform(streams_of[0], (GROUPS, LEN, HEADS * HEAD_DIM), jnp.float32, -1.7265625, 1.7265625) * block_levels(streams_of[0], (GROUPS, LEN, HEADS * HEAD_DIM), ((0, 16), (2, 2)), -0.4, 0.0), -1.7265625, 1.7265625).astype(jnp.bfloat16),
        "key": jnp.clip(jax.random.uniform(streams_of[1], (GROUPS, LEN, HEADS * HEAD_DIM), jnp.float32, -1.7265625, 1.7265625) * block_levels(streams_of[1], (GROUPS, LEN, HEADS * HEAD_DIM), ((0, 16), (2, 2)), -0.4, 0.0), -1.7265625, 1.7265625).astype(jnp.bfloat16),
        "value": centred(streams_of[2], (GROUPS, LEN, HEADS * HEAD_DIM), 1.0, 6.0, ((0, 16), (2, 2))),
        "output": centred(streams_of[3], (GROUPS, LEN, HEADS * HEAD_DIM), 0.25, 1.5, ((0, 16), (2, 2))),
        "grad_out": centred(streams_of[4], (GROUPS, LEN, HEADS * HEAD_DIM), (1.25 * LEN ** 0.5), 169.0, ((0, 16), (1, 2))),
        "log_sum": draw_log_sum(jax.random.fold_in(streams_of[8], 71), 0),
        "group_length": draw_group_length(jax.random.fold_in(streams_of[8], 71), 0),
        "cache_source": draw_cache_source(jax.random.fold_in(streams_of[8], 71), 0),
    }


def tile_grads(query_rows, grad_rows, lse_row, delta_row, key_rows, value_rows, alive_mask):
    score_scale = query_rows.shape[-1] ** -0.5
    scores = jnp.dot(query_rows, key_rows.T, preferred_element_type=jnp.float32) * score_scale
    attn_prob = jnp.where(alive_mask, jnp.exp(scores - lse_row[:, None]), 0.0)
    prob_half = attn_prob.astype(jnp.bfloat16)
    grad_prob = jnp.dot(grad_rows, value_rows.T, preferred_element_type=jnp.float32)
    grad_score = (attn_prob * (grad_prob - delta_row[:, None])).astype(jnp.bfloat16)
    grad_v = jnp.dot(prob_half.T, grad_rows, preferred_element_type=jnp.float32)
    grad_k = jnp.dot(grad_score.T, query_rows, preferred_element_type=jnp.float32) * score_scale
    grad_q = jnp.dot(grad_score, key_rows, preferred_element_type=jnp.float32) * score_scale
    return grad_q, grad_k, grad_v


def head_major(block):
    return block.reshape(LEN, HEADS, HEAD_DIM).transpose(1, 0, 2)


def token_major(block):
    return block.transpose(1, 0, 2).reshape(LEN, HEADS * HEAD_DIM)


def reference(query, key, value, output, grad_out, log_sum, group_length, cache_source):
    group_ids = jnp.arange(GROUPS, dtype=jnp.int32)
    linked = cache_source == group_ids - 1
    prev_length = jnp.concatenate([jnp.zeros((1,), jnp.int32), group_length[:-1]])
    prev_key = jnp.concatenate([jnp.zeros_like(key[:1]), key[:-1]], axis=0)
    prev_value = jnp.concatenate([jnp.zeros_like(value[:1]), value[:-1]], axis=0)
    row_index = jnp.arange(LEN, dtype=jnp.int32)

    def step(carry, inputs):
        carry_k, carry_v = carry
        q_c, k_c, v_c, o_c, g_c, lse_c, pk_c, pv_c, own_len, prev_len, link_c = inputs
        row_delta = jnp.sum((g_c.astype(jnp.float32) * o_c.astype(jnp.float32)).reshape(LEN, HEADS, HEAD_DIM), axis=2).T
        own_rows = row_index < own_len
        self_mask = own_rows[:, None] & own_rows[None, :]
        cross_mask = own_rows[:, None] & ((row_index < prev_len) & link_c)[None, :]

        def per_head(items):
            qh, gh, lh, dh, kh, vh, pkh, pvh = items
            sq, sk, sv = tile_grads(qh, gh, lh, dh, kh, vh, self_mask)
            xq, xk, xv = tile_grads(qh, gh, lh, dh, pkh, pvh, cross_mask)
            return sq + xq, sk, sv, xk, xv

        hq, hk, hv, hxk, hxv = lax.map(per_head, (head_major(q_c), head_major(g_c), lse_c, row_delta, head_major(k_c), head_major(v_c), head_major(pk_c), head_major(pv_c)))
        out_q = token_major(hq).astype(jnp.bfloat16)
        out_k = (token_major(hk) + carry_k).astype(jnp.bfloat16)
        out_v = (token_major(hv) + carry_v).astype(jnp.bfloat16)
        return (token_major(hxk), token_major(hxv)), (out_q, out_k, out_v)

    start = (jnp.zeros((LEN, HEADS * HEAD_DIM), jnp.float32), jnp.zeros((LEN, HEADS * HEAD_DIM), jnp.float32))
    _, outs = lax.scan(step, start, (query, key, value, output, grad_out, log_sum, prev_key, prev_value, group_length, prev_length, linked), reverse=True)
    return outs[0], outs[1], outs[2]
```

```python
import functools
import math

import jax
import jax.numpy as jnp
from jax import lax
from jax.experimental import pallas as pl
from jax.experimental.pallas import tpu as pltpu
from jax.sharding import PartitionSpec as P

HEAD_DIM = 128
STAT_ROWS = 32
DEAD = 1e30
LOG2E = 1.4426950408889634


def shifted(block, axis, distance):
    size = lax.axis_size(axis)
    return lax.ppermute(block, axis, [(i, (i + distance) % size) for i in range(size)])


def passed_along(block, axis, distance):
    devices = range(lax.axis_size(axis))
    route = [(i - distance, i) for i in devices if i - distance in devices]
    return lax.ppermute(block, axis, route)


def chunks_of(head_count):
    if head_count == 20:
        return (2, 4, 5, 5, 4)
    return (1,) * min(head_count, 4) + ((head_count - 4,) if head_count > 4 else ())


def three_parts(x):
    high = x.astype(jnp.bfloat16)
    rest = x - high.astype(jnp.float32)
    mid = rest.astype(jnp.bfloat16)
    low = (rest - mid.astype(jnp.float32)).astype(jnp.bfloat16)
    return high, mid, low


def pack_kernel(scalars, grad_own, grad_recv, out, query, lse, packed, grads, *, first):
    me = scalars[0]
    rows = query.shape[0]
    per = grad_own.shape[0]
    size = rows // per
    packed[0, :rows, :] = query[...]
    for r in range(size):
        start = pl.multiple_of(lax.rem(me - r + size, size) * per, per)
        block = grad_own[...] if r == 0 else grad_recv[r - 1]
        packed[0, pl.ds(pl.multiple_of(rows + start, per), per), :] = block
        grads[pl.ds(start, per), :] = block
    product = grads[...].astype(jnp.float32) * out[...].astype(jnp.float32)
    delta = lax.dot_general(
        jnp.ones((8, HEAD_DIM), jnp.float32),
        product,
        (((1,), (1,)), ((), ())),
        precision=lax.Precision.HIGHEST,
        preferred_element_type=jnp.float32,
    )[:1]
    head = first + pl.program_id(0)
    log_sum = lse[pl.ds(head, 1), :] * LOG2E
    parts = three_parts(delta) + three_parts(log_sum)
    lanes = rows // HEAD_DIM
    pieces = [
        part[:, j * HEAD_DIM : (j + 1) * HEAD_DIM].astype(jnp.float32)
        for part in parts
        for j in range(lanes)
    ]
    pieces.append(jnp.zeros((STAT_ROWS - len(pieces), HEAD_DIM), jnp.float32))
    packed[0, 2 * rows :, :] = jnp.concatenate(pieces, axis=0).astype(jnp.bfloat16)


def pack(scalars, grad, grad_recv, out, query, lse, first, count):
    rows = query.shape[0]
    per = grad.shape[0]
    size = rows // per
    heads = query.shape[1] // HEAD_DIM
    height = 2 * rows + STAT_ROWS
    return pl.pallas_call(
        functools.partial(pack_kernel, first=first),
        grid_spec=pltpu.PrefetchScalarGridSpec(
            num_scalar_prefetch=1,
            grid=(count,),
            in_specs=[
                pl.BlockSpec((per, HEAD_DIM), lambda h, s: (0, s[0] * heads + first + h)),
                pl.BlockSpec((size - 1, per, HEAD_DIM), lambda h, s: (0, 0, h)),
                pl.BlockSpec((rows, HEAD_DIM), lambda h, s: (0, first + h)),
                pl.BlockSpec((rows, HEAD_DIM), lambda h, s: (0, first + h)),
                pl.BlockSpec(lse.shape, lambda h, s: (0, 0)),
            ],
            out_specs=pl.BlockSpec((1, height, HEAD_DIM), lambda h, s: (h, 0, 0)),
            scratch_shapes=[pltpu.VMEM((rows, HEAD_DIM), jnp.bfloat16)],
        ),
        out_shape=jax.ShapeDtypeStruct((count, height, HEAD_DIM), jnp.bfloat16),
        cost_estimate=pl.CostEstimate(
            flops=count * rows * HEAD_DIM * 16,
            bytes_accessed=count * rows * HEAD_DIM * 10,
            transcendentals=0,
        ),
        name="pack",
    )(scalars, grad, grad_recv, out, query, lse)


def stat_row(stats, at, lanes):
    total = (
        stats[at : at + lanes] + stats[at + lanes : at + 2 * lanes]
    ) + stats[at + 2 * lanes : at + 3 * lanes]
    return jnp.concatenate([total[j : j + 1] for j in range(lanes)], axis=1)


def block_grads(key, key_t, value, packed, query_len):
    rows = key.shape[0]
    lanes = rows // HEAD_DIM
    scale = HEAD_DIM**-0.5
    query = packed[0, :rows, :]
    grad = packed[0, rows : 2 * rows, :]
    stats = packed[0, 2 * rows :, :].astype(jnp.float32)
    delta = stat_row(stats, 0, lanes)
    log_sum = stat_row(stats, 3 * lanes, lanes)
    alive = lax.broadcasted_iota(jnp.int32, (1, rows), 1) < query_len
    log_sum = jnp.where(alive, log_sum, DEAD)
    across = (((1,), (1,)), ((), ()))
    tile = min(256, rows)
    dks, dvs, dq_t = [], [], None
    for at in range(0, rows, tile):
        scores = lax.dot_general(
            key[at : at + tile], query, across, preferred_element_type=jnp.float32
        )
        prob = jnp.exp2(scores * (scale * LOG2E) - log_sum)
        grad_prob = lax.dot_general(
            value[at : at + tile], grad, across, preferred_element_type=jnp.float32
        )
        grad_score = (prob * (grad_prob - delta)).astype(jnp.bfloat16)
        dvs.append(
            jnp.dot(prob.astype(jnp.bfloat16), grad, preferred_element_type=jnp.float32)
        )
        dks.append(jnp.dot(grad_score, query, preferred_element_type=jnp.float32))
        part = jnp.dot(
            key_t[:, at : at + tile], grad_score, preferred_element_type=jnp.float32
        )
        dq_t = part if dq_t is None else dq_t + part
    return dq_t, jnp.concatenate(dks, axis=0), jnp.concatenate(dvs, axis=0)


def grads_kernel(scalars, *refs, carried):
    key, value, own, following = refs[:4]
    refs = refs[4 + carried :]
    key_out, value_out, send, query_own, query_cross, both = refs
    me, own_len, cross_len = scalars[0], scalars[1], scalars[2]
    rows = key.shape[0]
    per = key_out.shape[0]
    size = rows // per
    scale = HEAD_DIM**-0.5
    live = lax.broadcasted_iota(jnp.int32, (rows, 1), 0) < own_len
    k, v = key[...], value[...]
    masked = jnp.where(live, k.astype(jnp.float32), 0.0)
    key_t = masked.T.astype(jnp.bfloat16)
    dq, dk, dv = block_grads(k, key_t, v, own, own_len)
    query_own[0] = dq.T * scale
    xq, xk, xv = block_grads(k, key_t, v, following, cross_len)
    query_cross[0] = (xq.T * scale).astype(jnp.bfloat16)
    both[0] = jnp.where(live, (dk + xk) * scale, 0.0).astype(jnp.bfloat16)
    both[1] = jnp.where(live, dv + xv, 0.0).astype(jnp.bfloat16)
    for r in range(size):
        start = pl.multiple_of(lax.rem(me - r + size, size) * per, per)
        if r == 0:
            key_out[...] = both[0, pl.ds(start, per), :]
            value_out[...] = both[1, pl.ds(start, per), :]
        else:
            send[r - 1, 0] = both[0, pl.ds(start, per), :]
            send[r - 1, 1] = both[1, pl.ds(start, per), :]


def grads(scalars, key, value, own, following, carried, size, first, count):
    rows, width = key.shape
    per = rows // size
    heads = width // HEAD_DIM
    height = own.shape[1]
    any_spec = pl.BlockSpec(memory_space=pl.ANY)
    own_spec = pl.BlockSpec((per, HEAD_DIM), lambda h, s: (0, s[0] * heads + first + h))
    full = jax.ShapeDtypeStruct((per, width * size), jnp.bfloat16)
    return pl.pallas_call(
        functools.partial(grads_kernel, carried=len(carried)),
        grid_spec=pltpu.PrefetchScalarGridSpec(
            num_scalar_prefetch=1,
            grid=(count,),
            in_specs=[
                pl.BlockSpec((rows, HEAD_DIM), lambda h, s: (0, first + h)),
                pl.BlockSpec((rows, HEAD_DIM), lambda h, s: (0, first + h)),
                pl.BlockSpec((1, height, HEAD_DIM), lambda h, s: (h, 0, 0)),
                pl.BlockSpec((1, height, HEAD_DIM), lambda h, s: (h, 0, 0)),
            ]
            + [any_spec] * len(carried),
            out_specs=[
                own_spec,
                own_spec,
                pl.BlockSpec((size - 1, 2, per, HEAD_DIM), lambda h, s: (0, 0, 0, h)),
                pl.BlockSpec((1, rows, HEAD_DIM), lambda h, s: (h, 0, 0)),
                pl.BlockSpec((1, rows, HEAD_DIM), lambda h, s: (h, 0, 0)),
            ],
            scratch_shapes=[pltpu.VMEM((2, rows, HEAD_DIM), jnp.bfloat16)],
        ),
        out_shape=[
            full,
            full,
            jax.ShapeDtypeStruct((size - 1, 2, per, count * HEAD_DIM), jnp.bfloat16),
            jax.ShapeDtypeStruct((count, rows, HEAD_DIM), jnp.float32),
            jax.ShapeDtypeStruct((count, rows, HEAD_DIM), jnp.bfloat16),
        ],
        input_output_aliases={5 + i: i for i in range(len(carried))},
        cost_estimate=pl.CostEstimate(
            flops=count * 20 * rows * rows * HEAD_DIM,
            bytes_accessed=count * rows * HEAD_DIM * 24,
            transcendentals=count * 2 * rows * rows,
        ),
        name="grads",
    )(scalars, key, value, own, following, *carried)


def query_kernel(scalars, own, back, *refs, carried):
    query_out, send, total = refs[carried:]
    me = scalars[0]
    rows = own.shape[1]
    per = query_out.shape[0]
    size = rows // per
    total[...] = (own[0] + back[0].astype(jnp.float32)).astype(jnp.bfloat16)
    for r in range(size):
        start = pl.multiple_of(lax.rem(me - r + size, size) * per, per)
        if r == 0:
            query_out[...] = total[pl.ds(start, per), :]
        else:
            send[r - 1] = total[pl.ds(start, per), :]


def query_sum(scalars, own, back, carried, size, heads, first):
    count, rows, _ = own.shape
    per = rows // size
    any_spec = pl.BlockSpec(memory_space=pl.ANY)
    return pl.pallas_call(
        functools.partial(query_kernel, carried=len(carried)),
        grid_spec=pltpu.PrefetchScalarGridSpec(
            num_scalar_prefetch=1,
            grid=(count,),
            in_specs=[
                pl.BlockSpec((1, rows, HEAD_DIM), lambda h, s: (h, 0, 0)),
                pl.BlockSpec((1, rows, HEAD_DIM), lambda h, s: (h, 0, 0)),
            ]
            + [any_spec] * len(carried),
            out_specs=[
                pl.BlockSpec((per, HEAD_DIM), lambda h, s: (0, s[0] * heads + first + h)),
                pl.BlockSpec((size - 1, per, HEAD_DIM), lambda h, s: (0, 0, h)),
            ],
            scratch_shapes=[pltpu.VMEM((rows, HEAD_DIM), jnp.bfloat16)],
        ),
        out_shape=[
            jax.ShapeDtypeStruct((per, heads * size * HEAD_DIM), jnp.bfloat16),
            jax.ShapeDtypeStruct((size - 1, per, count * HEAD_DIM), jnp.bfloat16),
        ],
        input_output_aliases={3 + i: i for i in range(len(carried))},
        cost_estimate=pl.CostEstimate(
            flops=count * rows * HEAD_DIM,
            bytes_accessed=count * rows * HEAD_DIM * 8,
            transcendentals=0,
        ),
        name="query_sum",
    )(scalars, own, back, *carried)


def place_kernel(scalars, *refs, plan, targets, size, heads):
    blocks = refs[: len(plan)]
    outs = refs[len(plan) + targets : len(plan) + 2 * targets]
    sems = refs[-1]
    me = scalars[0]
    copies = []
    for block, (rel, first, dests) in zip(blocks, plan):
        peer = lax.rem(me + rel, size)
        width = block.shape[-1]
        column = pl.multiple_of((peer * heads + first) * HEAD_DIM, HEAD_DIM)
        for j, dest in enumerate(dests):
            copies.append(
                pltpu.make_async_copy(
                    block.at[j], outs[dest].at[:, pl.ds(column, width)], sems.at[len(copies)]
                )
            )
    for copy in copies:
        copy.start()
    for copy in copies:
        copy.wait()


def place(scalars, blocks, plan, outs, size, heads):
    any_spec = pl.BlockSpec(memory_space=pl.ANY)
    copies = sum(len(dests) for _, _, dests in plan)
    return pl.pallas_call(
        functools.partial(
            place_kernel, plan=plan, targets=len(outs), size=size, heads=heads
        ),
        grid_spec=pltpu.PrefetchScalarGridSpec(
            num_scalar_prefetch=1,
            grid=(1,),
            in_specs=[
                pl.BlockSpec(b.shape, functools.partial(lambda n, i, s: (0,) * n, b.ndim))
                for b in blocks
            ]
            + [any_spec] * len(outs),
            out_specs=[any_spec] * len(outs),
            scratch_shapes=[pltpu.SemaphoreType.DMA((copies,))],
        ),
        out_shape=[jax.ShapeDtypeStruct(o.shape, o.dtype) for o in outs],
        input_output_aliases={1 + len(blocks) + i: i for i in range(len(outs))},
        cost_estimate=pl.CostEstimate(
            flops=0,
            bytes_accessed=sum(4 * math.prod(b.shape) for b in blocks),
            transcendentals=0,
        ),
        name="place",
    )(scalars, *blocks, *outs)


def lookup_at(table, group_ids, target):
    return jnp.sum(jnp.where(group_ids == target, table, 0))


def on_device(query, key, value, output, grad_out, log_sum, group_length, cache_source):
    size = lax.axis_size("head")
    me = lax.axis_index("head")
    group_at = lax.axis_index("group")
    query, key, value, output = query[0], key[0], value[0], output[0]
    grad, lse = grad_out[0], log_sum[0]
    width = query.shape[1]
    heads = width // HEAD_DIM
    counts = chunks_of(heads)
    firsts = [sum(counts[:i]) for i in range(len(counts))]

    group_ids = jnp.arange(group_length.shape[0], dtype=jnp.int32)
    linked = (cache_source == group_ids - 1).astype(jnp.int32)
    own_len = lookup_at(group_length, group_ids, group_at)
    next_len = lookup_at(group_length, group_ids, group_at + 1)
    next_link = lookup_at(linked, group_ids, group_at + 1)
    scalars = jnp.stack([me, own_len, next_len * next_link, group_at]).astype(jnp.int32)

    received = []
    for first, count in zip(firsts, counts):
        blocks = []
        for rel in range(1, size):
            peer = lax.rem(me + rel, size)
            start = (peer * heads + first) * HEAD_DIM
            block = lax.dynamic_slice_in_dim(grad, start, count * HEAD_DIM, axis=1)
            blocks.append(shifted(block, "head", rel)[None])
        received.append(blocks[0] if size == 2 else jnp.concatenate(blocks, axis=0))

    packs, nexts = [], []
    for i, (first, count) in enumerate(zip(firsts, counts)):
        packs.append(pack(scalars, grad, received[i], output, query, lse, first, count))
        nexts.append(passed_along(packs[i], "group", -1))

    kv_outs, q_outs = (), ()
    kv_blocks, kv_plan, q_blocks, q_plan = [], [], [], []
    for i, (first, count) in enumerate(zip(firsts, counts)):
        key_out, value_out, kv_send, q_own, q_cross = grads(
            scalars, key, value, packs[i], nexts[i], kv_outs, size, first, count
        )
        kv_outs = (key_out, value_out)
        for rel in range(1, size):
            kv_blocks.append(shifted(kv_send[rel - 1], "head", -rel))
            kv_plan.append((rel, first, (0, 1)))
        back = passed_along(q_cross, "group", 1)
        query_out, q_send = query_sum(scalars, q_own, back, q_outs, size, heads, first)
        q_outs = (query_out,)
        for rel in range(1, size):
            q_blocks.append(shifted(q_send[rel - 1][None], "head", -rel))
            q_plan.append((rel, first, (0,)))

    key_out, value_out = place(scalars, kv_blocks, tuple(kv_plan), kv_outs, size, heads)
    last = size - 1
    (query_out,) = place(scalars, q_blocks[:-last], tuple(q_plan[:-last]), q_outs, size, heads)
    (query_out,) = place(
        scalars, q_blocks[-last:], tuple(q_plan[-last:]), (query_out,), size, heads
    )
    return query_out[None], key_out[None], value_out[None]


def solution(mesh):
    in_specs = (
        P("group", None, "head"),
        P("group", None, "head"),
        P("group", None, "head"),
        P("group", None, "head"),
        P("group", "head", None),
        P("group", "head", None),
        P(),
        P(),
    )
    out_specs = (P("group", "head", None), P("group", "head", None), P("group", "head", None))
    return jax.shard_map(
        on_device, mesh=mesh, in_specs=in_specs, out_specs=out_specs, check_vma=False
    )
```

```python
import functools
import math

import jax
import jax.numpy as jnp
from jax import lax
from jax.experimental import pallas as pl
from jax.experimental.pallas import tpu as pltpu
from jax.sharding import PartitionSpec as P


HEAD_DIM = 128
STAT_ROWS = 32
DEAD = 1e30
LOG2E = 1.4426950408889634
VMEM_LIMIT = 24 * 1024 * 1024
KEY_TILE = 512
CHUNKS = (3, 5, 5, 4, 3)


def shifted(block, axis, distance):
    size = lax.axis_size(axis)
    return lax.ppermute(block, axis, [(i, (i + distance) % size) for i in range(size)])


def passed_along(block, axis, distance):
    devices = range(lax.axis_size(axis))
    route = [(i - distance, i) for i in devices if i - distance in devices]
    return lax.ppermute(block, axis, route)


def chunks_of(head_count):
    if head_count == 20:
        return CHUNKS
    return (1,) * min(head_count, 4) + ((head_count - 4,) if head_count > 4 else ())


def moves_of(chunks):
    return [(0, 1)[:chunks]]


def groups_of(chunks):
    groups = [(0, 1)[:chunks], tuple(range(2, chunks - 1)), tuple(range(max(2, chunks - 1), chunks))]
    return [group for group in groups if group]


def three_parts(x):
    high = x.astype(jnp.bfloat16)
    rest = x - high.astype(jnp.float32)
    mid = rest.astype(jnp.bfloat16)
    low = (rest - mid.astype(jnp.float32)).astype(jnp.bfloat16)
    return high, mid, low


def cut_kernel(grad, query, *refs, plan, heads):
    outs, sems = refs[:-1], refs[-1]
    size = grad.shape[1] // query.shape[1]
    copies = []
    for i, (out, (rel, first)) in enumerate(zip(outs, plan)):
        source, column = query, first * HEAD_DIM
        if rel:
            peer = lax.rem(lax.axis_index("head") + rel, size)
            source, column = grad, (peer * heads + first) * HEAD_DIM
        column = pl.multiple_of(column, HEAD_DIM)
        copies.append(
            pltpu.make_async_copy(source.at[:, pl.ds(column, out.shape[1])], out, sems.at[i])
        )
    for copy in copies:
        copy.start()
    for copy in copies:
        copy.wait()


def cut(grad, query, plan, counts):
    heads = query.shape[1] // HEAD_DIM
    any_spec = pl.BlockSpec(memory_space=pltpu.HBM)
    shapes = [
        ((grad if rel else query).shape[0], count * HEAD_DIM)
        for (rel, _), count in zip(plan, counts)
    ]
    return pl.pallas_call(
        functools.partial(cut_kernel, plan=plan, heads=heads),
        grid=(1,),
        in_specs=[any_spec, any_spec],
        out_specs=[pl.BlockSpec(shape, lambda i: (0, 0)) for shape in shapes],
        out_shape=[jax.ShapeDtypeStruct(shape, jnp.bfloat16) for shape in shapes],
        scratch_shapes=[pltpu.SemaphoreType.DMA((len(plan),))],
        cost_estimate=pl.CostEstimate(
            flops=0,
            bytes_accessed=sum(4 * math.prod(shape) for shape in shapes),
            transcendentals=0,
        ),
        name="cut",
    )(grad, query)


def pack_kernel(grad, grad_recv, out, lse, query, packed, *scratch, first):
    me = lax.axis_index("head")
    count, height, _ = packed.shape
    rows = out.shape[0]
    top = height - rows - STAT_ROWS
    (grad_own, out_own), sems = scratch[:2], scratch[-1]
    per = grad.shape[0]
    size = rows // per
    lanes = rows // HEAD_DIM
    width = count * HEAD_DIM
    heads = out.shape[1] // HEAD_DIM
    column = pl.multiple_of((me * heads + first) * HEAD_DIM, HEAD_DIM)
    copies = [
        pltpu.make_async_copy(grad.at[:, pl.ds(column, width)], grad_own, sems.at[0]),
        pltpu.make_async_copy(out.at[:, pl.ds(first * HEAD_DIM, width)], out_own, sems.at[1]),
    ]
    if top:
        copies.append(
            pltpu.make_async_copy(
                query.at[:, pl.ds(first * HEAD_DIM, width)], scratch[2], sems.at[2]
            )
        )
    for copy in copies:
        copy.start()
    for copy in copies:
        copy.wait()
    ones = jnp.ones((16, HEAD_DIM), jnp.bfloat16)
    for h in range(count):
        cols = slice(h * HEAD_DIM, (h + 1) * HEAD_DIM)
        for r in range(size):
            start = pl.multiple_of(lax.rem(me - r + size, size) * per, per)
            block = grad_own[:, cols] if r == 0 else grad_recv[r - 1, :, cols]
            packed[h, pl.ds(pl.multiple_of(top + start, per), per), :] = block
        if top:
            packed[h, :top, :] = scratch[2][:, cols]
        product = packed[h, top : top + rows].astype(jnp.float32) * out_own[:, cols].astype(jnp.float32)
        delta = sum(
            lax.dot_general(
                ones, part, (((1,), (1,)), ((), ())), preferred_element_type=jnp.float32
            )
            for part in three_parts(product)
        )[:1]
        log_sum = lse[first + h : first + h + 1, :] * LOG2E
        parts = three_parts(delta) + three_parts(log_sum)
        pieces = [
            part[:, j * HEAD_DIM : (j + 1) * HEAD_DIM].astype(jnp.float32)
            for part in parts
            for j in range(lanes)
        ]
        pieces.append(jnp.zeros((STAT_ROWS - len(pieces), HEAD_DIM), jnp.float32))
        packed[h, top + rows :, :] = jnp.concatenate(pieces, axis=0).astype(jnp.bfloat16)


def pack(grad, grad_recv, out, lse, query, first, count, joined):
    rows = out.shape[0]
    per = grad.shape[0]
    height = rows * (1 + joined) + STAT_ROWS
    width = count * HEAD_DIM
    any_spec = pl.BlockSpec(memory_space=pltpu.HBM if first == 0 else pl.ANY)
    return pl.pallas_call(
        functools.partial(pack_kernel, first=first),
        grid_spec=pltpu.PrefetchScalarGridSpec(
            num_scalar_prefetch=0,
            grid=(1,),
            in_specs=[
                any_spec,
                pl.BlockSpec(grad_recv.shape, lambda i: (0, 0, 0)),
                any_spec,
                pl.BlockSpec(lse.shape, lambda i: (0, 0)),
                any_spec,
            ],
            out_specs=pl.BlockSpec((count, height, HEAD_DIM), lambda i: (0, 0, 0)),
            scratch_shapes=[
                pltpu.VMEM((per, width), jnp.bfloat16),
                pltpu.VMEM((rows, width), jnp.bfloat16),
            ]
            + [pltpu.VMEM((rows, width), jnp.bfloat16)] * joined
            + [pltpu.SemaphoreType.DMA((2 + joined,))],
        ),
        out_shape=jax.ShapeDtypeStruct((count, height, HEAD_DIM), jnp.bfloat16),
        compiler_params=pltpu.CompilerParams(vmem_limit_bytes=VMEM_LIMIT),
        cost_estimate=pl.CostEstimate(
            flops=count * rows * HEAD_DIM * 16,
            bytes_accessed=count * rows * HEAD_DIM * 6,
            transcendentals=0,
        ),
        name="pack",
    )(grad, grad_recv, out, lse, query)


def stat_row(stats, at, lanes):
    total = (
        stats[at : at + lanes] + stats[at + lanes : at + 2 * lanes]
    ) + stats[at + 2 * lanes : at + 3 * lanes]
    return jnp.concatenate([total[j : j + 1] for j in range(lanes)], axis=1)


def stat_rows(packed, rows, query_len):
    lanes = rows // HEAD_DIM
    stats = packed[0, packed.shape[1] - STAT_ROWS :, :].astype(jnp.float32)
    alive = lax.broadcasted_iota(jnp.int32, (1, rows), 1) < query_len
    log_sum = jnp.where(alive, stat_row(stats, 3 * lanes, lanes), DEAD)
    return stat_row(stats, 0, lanes), log_sum


def grads_kernel(lengths, sources, *refs, carried, tile):
    key, value, query, own, next_query, following = refs[:6]
    refs = refs[6 + carried :]
    key_out, value_out, send, query_own, query_cross, both = refs
    me, group_at = lax.axis_index("head"), lax.axis_index("group")
    own_len = lengths[group_at]
    after = lax.min(group_at + 1, lengths.shape[0] - 1)
    linked = (group_at + 1 == after) & (sources[after] == group_at)
    cross_len = jnp.where(linked, lengths[after], 0)
    rows = key.shape[0]
    per = key_out.shape[0]
    size = rows // per
    scale = HEAD_DIM**-0.5
    across = (((1,), (1,)), ((), ()))
    key_t = key[...].astype(jnp.float32).T
    live_t = lax.broadcasted_iota(jnp.int32, (1, rows), 1) < own_len
    key_t = jnp.where(live_t, key_t, 0.0).astype(jnp.bfloat16)
    delta, log_sum = zip(
        stat_rows(own, rows, own_len), stat_rows(following, rows, cross_len)
    )
    top = own.shape[1] - rows - STAT_ROWS
    queries = (query[...], following[0, :rows, :] if top else next_query[...])
    grad = (own[0, top : top + rows, :], following[0, top : top + rows, :])
    all_queries, all_grad = jnp.concatenate(queries, axis=0), jnp.concatenate(grad, axis=0)
    dq_t = None
    for at in range(0, rows, tile):
        k, v = key[at : at + tile, :], value[at : at + tile, :]
        probs, grad_scores = [], []
        for i in range(2):
            scores = lax.dot_general(k, queries[i], across, preferred_element_type=jnp.float32)
            prob = jnp.exp2(scores * (scale * LOG2E) - log_sum[i])
            grad_prob = lax.dot_general(v, grad[i], across, preferred_element_type=jnp.float32)
            grad_scores.append((prob * (grad_prob - delta[i])).astype(jnp.bfloat16))
            probs.append(prob.astype(jnp.bfloat16))
        probs = jnp.concatenate(probs, axis=1)
        grad_scores = jnp.concatenate(grad_scores, axis=1)
        dv = jnp.dot(probs, all_grad, preferred_element_type=jnp.float32)
        dk = jnp.dot(grad_scores, all_queries, preferred_element_type=jnp.float32)
        live = lax.broadcasted_iota(jnp.int32, (tile, 1), 0) + at < own_len
        both[0, at : at + tile, :] = jnp.where(live, dk * scale, 0.0).astype(jnp.bfloat16)
        both[1, at : at + tile, :] = jnp.where(live, dv, 0.0).astype(jnp.bfloat16)
        part = jnp.dot(
            key_t[:, at : at + tile], grad_scores, preferred_element_type=jnp.float32
        )
        dq_t = part if dq_t is None else dq_t + part
    query_own[0] = dq_t[:, :rows].T * scale
    query_cross[0] = (dq_t[:, rows:].T * scale).astype(jnp.bfloat16)
    for r in range(size):
        start = pl.multiple_of(lax.rem(me - r + size, size) * per, per)
        if r == 0:
            key_out[...] = both[0, pl.ds(start, per), :]
            value_out[...] = both[1, pl.ds(start, per), :]
        else:
            send[r - 1, 0] = both[0, pl.ds(start, per), :]
            send[r - 1, 1] = both[1, pl.ds(start, per), :]


def grads(
    lengths, sources, key, value, query, own, next_query, next_first, following, carried, aliases,
    size, first, count, base, total,
):
    rows, width = key.shape
    per = rows // size
    heads = width // HEAD_DIM
    height = own.shape[1]
    any_spec = pl.BlockSpec(memory_space=pl.ANY)
    own_spec = pl.BlockSpec((per, HEAD_DIM), lambda h, *_: (0, lax.axis_index("head") * heads + first + h))
    full = jax.ShapeDtypeStruct((per, width * size), jnp.bfloat16)
    return pl.pallas_call(
        functools.partial(grads_kernel, carried=len(carried), tile=min(KEY_TILE, rows)),
        grid_spec=pltpu.PrefetchScalarGridSpec(
            num_scalar_prefetch=2,
            grid=(count,),
            in_specs=[
                pl.BlockSpec((rows, HEAD_DIM), lambda h, *_: (0, first + h)),
                pl.BlockSpec((rows, HEAD_DIM), lambda h, *_: (0, first + h)),
                pl.BlockSpec((rows, HEAD_DIM), lambda h, *_: (0, first + h)),
                pl.BlockSpec((1, height, HEAD_DIM), lambda h, *_: (h, 0, 0)),
                pl.BlockSpec((rows, HEAD_DIM), lambda h, *_: (0, first - next_first + h))
                if height == rows + STAT_ROWS
                else any_spec,
                pl.BlockSpec((1, height, HEAD_DIM), lambda h, *_: (h, 0, 0)),
            ]
            + [any_spec] * len(carried),
            out_specs=[
                own_spec,
                own_spec,
                pl.BlockSpec((size - 1, 2, per, HEAD_DIM), lambda h, *_: (0, 0, 0, h)),
                pl.BlockSpec((1, rows, HEAD_DIM), lambda h, *_: (base + h, 0, 0)),
                pl.BlockSpec((1, rows, HEAD_DIM), lambda h, *_: (base + h, 0, 0)),
            ],
            scratch_shapes=[pltpu.VMEM((2, rows, HEAD_DIM), jnp.bfloat16)],
        ),
        out_shape=[
            full,
            full,
            jax.ShapeDtypeStruct((size - 1, 2, per, count * HEAD_DIM), jnp.bfloat16),
            jax.ShapeDtypeStruct((total, rows, HEAD_DIM), jnp.float32),
            jax.ShapeDtypeStruct((total, rows, HEAD_DIM), jnp.bfloat16),
        ],
        input_output_aliases={8 + i: out for i, out in enumerate(aliases)},
        compiler_params=pltpu.CompilerParams(vmem_limit_bytes=VMEM_LIMIT),
        cost_estimate=pl.CostEstimate(
            flops=count * 20 * rows * rows * HEAD_DIM,
            bytes_accessed=count * rows * HEAD_DIM * 24,
            transcendentals=count * 2 * rows * rows,
        ),
        name="grads",
    )(lengths, sources, key, value, query, own, next_query, following, *carried)


def query_kernel(own, back, *refs, carried, first, heads):
    query_out, send, total, sem = refs[carried:]
    me = lax.axis_index("head")
    count, rows, _ = own.shape
    per = query_out.shape[0]
    size = rows // per
    for h in range(count):
        cols = slice(h * HEAD_DIM, (h + 1) * HEAD_DIM)
        total[:, cols] = (own[h] + back[h].astype(jnp.float32)).astype(jnp.bfloat16)
    column = pl.multiple_of((me * heads + first) * HEAD_DIM, HEAD_DIM)
    start = pl.multiple_of(me * per, per)
    copy = pltpu.make_async_copy(
        total.at[pl.ds(start, per), :],
        query_out.at[:, pl.ds(column, count * HEAD_DIM)],
        sem.at[0],
    )
    copy.start()
    for r in range(1, size):
        start = pl.multiple_of(lax.rem(me - r + size, size) * per, per)
        send[r - 1] = total[pl.ds(start, per), :]
    copy.wait()


def query_sum(own, back, carried, size, heads, first):
    count, rows, _ = own.shape
    per = rows // size
    any_spec = pl.BlockSpec(memory_space=pl.ANY)
    whole = (count, rows, HEAD_DIM)
    return pl.pallas_call(
        functools.partial(query_kernel, carried=len(carried), first=first, heads=heads),
        grid_spec=pltpu.PrefetchScalarGridSpec(
            num_scalar_prefetch=0,
            grid=(1,),
            in_specs=[
                pl.BlockSpec(whole, lambda i: (0, 0, 0)),
                pl.BlockSpec(whole, lambda i: (0, 0, 0)),
            ]
            + [any_spec] * len(carried),
            out_specs=[
                any_spec,
                pl.BlockSpec((size - 1, per, count * HEAD_DIM), lambda i: (0, 0, 0)),
            ],
            scratch_shapes=[
                pltpu.VMEM((rows, count * HEAD_DIM), jnp.bfloat16),
                pltpu.SemaphoreType.DMA((1,)),
            ],
        ),
        out_shape=[
            jax.ShapeDtypeStruct((per, heads * size * HEAD_DIM), jnp.bfloat16),
            jax.ShapeDtypeStruct((size - 1, per, count * HEAD_DIM), jnp.bfloat16),
        ],
        input_output_aliases={2 + i: i for i in range(len(carried))},
        compiler_params=pltpu.CompilerParams(vmem_limit_bytes=VMEM_LIMIT),
        cost_estimate=pl.CostEstimate(
            flops=count * rows * HEAD_DIM,
            bytes_accessed=count * rows * HEAD_DIM * 8,
            transcendentals=0,
        ),
        name="query_sum",
    )(own, back, *carried)


def place_kernel(*refs, plan, targets, size, heads):
    blocks = refs[: len(plan)]
    outs = refs[len(plan) + targets : len(plan) + 2 * targets]
    sems = refs[-1]
    me = lax.axis_index("head")
    copies = []
    for block, (rel, first, dests) in zip(blocks, plan):
        peer = lax.rem(me + rel, size)
        width = block.shape[-1]
        column = pl.multiple_of((peer * heads + first) * HEAD_DIM, HEAD_DIM)
        for j, dest in enumerate(dests):
            copies.append(
                pltpu.make_async_copy(
                    block.at[j], outs[dest].at[:, pl.ds(column, width)], sems.at[len(copies)]
                )
            )
    for copy in copies:
        copy.start()
    for copy in copies:
        copy.wait()


def place(blocks, plan, outs, size, heads):
    any_spec = pl.BlockSpec(memory_space=pl.ANY)
    copies = sum(len(dests) for _, _, dests in plan)
    return pl.pallas_call(
        functools.partial(
            place_kernel, plan=plan, targets=len(outs), size=size, heads=heads
        ),
        grid_spec=pltpu.PrefetchScalarGridSpec(
            num_scalar_prefetch=0,
            grid=(1,),
            in_specs=[
                pl.BlockSpec(b.shape, functools.partial(lambda n, i: (0,) * n, b.ndim))
                for b in blocks
            ]
            + [any_spec] * len(outs),
            out_specs=[any_spec] * len(outs),
            scratch_shapes=[pltpu.SemaphoreType.DMA((copies,))],
        ),
        out_shape=[jax.ShapeDtypeStruct(o.shape, o.dtype) for o in outs],
        input_output_aliases={len(blocks) + i: i for i in range(len(outs))},
        compiler_params=pltpu.CompilerParams(vmem_limit_bytes=VMEM_LIMIT),
        cost_estimate=pl.CostEstimate(
            flops=0,
            bytes_accessed=sum(4 * math.prod(b.shape) for b in blocks),
            transcendentals=0,
        ),
        name="place",
    )(*blocks, *outs)


def on_device(query, key, value, output, grad_out, log_sum, group_length, cache_source):
    size = lax.axis_size("head")
    me = lax.axis_index("head")
    query, key, value, output = query[0], key[0], value[0], output[0]
    grad, lse = grad_out[0], log_sum[0]
    width = query.shape[1]
    heads = width // HEAD_DIM
    counts = chunks_of(heads)
    firsts = [sum(counts[:i]) for i in range(len(counts))]

    rels = range(1, size)
    moves = moves_of(len(counts))
    plan = [(rel, firsts[i]) for i in range(1, len(counts)) for rel in rels]
    widths = [counts[i] for i in range(1, len(counts)) for rel in rels]
    plan += [(0, firsts[group[0]]) for group in moves]
    widths += [sum(counts[i] for i in group) for group in moves]
    pieces = cut(grad, query, tuple(plan), widths)
    split = (len(counts) - 1) * (size - 1)
    pieces, query_blocks = list(pieces[:split]), pieces[split:]
    for rel in reversed(rels):
        start = (lax.rem(me + rel, size) * heads + firsts[0]) * HEAD_DIM
        block = lax.dynamic_slice_in_dim(grad, start, counts[0] * HEAD_DIM, axis=1)
        pieces = [block] + pieces

    received = []
    for i in range(len(counts)):
        blocks = []
        for rel in rels:
            blocks.append(shifted(pieces[i * (size - 1) + rel - 1], "head", rel)[None])
        received.append(blocks[0] if size == 2 else jnp.concatenate(blocks, axis=0))

    next_queries = {}
    for n, group in enumerate(moves):
        moved = passed_along(query_blocks[n], "group", -1)
        for i in group:
            next_queries[i] = (moved, firsts[group[0]])

    packs, nexts = [], []
    for i, (first, count) in enumerate(zip(firsts, counts)):
        joined = int(i not in next_queries)
        packs.append(pack(grad, received[i], output, lse, query, first, count, joined))
        nexts.append(passed_along(packs[i], "group", -1))

    kv_outs, q_outs = (), ()
    kv_blocks, kv_plan, q_blocks, q_plan = [], [], [], []
    for group in groups_of(len(counts)):
        total = sum(counts[i] for i in group)
        base, q_parts = 0, ()
        for i in group:
            aliases = ((0, 1) if kv_outs else ()) + ((3, 4) if q_parts else ())
            key_out, value_out, kv_send, q_own, q_cross = grads(
                group_length, cache_source, key, value, query, packs[i], *next_queries.get(i, (query, 0)), nexts[i],
                kv_outs + q_parts, aliases, size, firsts[i], counts[i], base, total,
            )
            kv_outs, q_parts = (key_out, value_out), (q_own, q_cross)
            base += counts[i]
            for rel in range(1, size):
                kv_blocks.append(shifted(kv_send[rel - 1], "head", -rel))
                kv_plan.append((rel, firsts[i], (0, 1)))
        back = passed_along(q_cross, "group", 1)
        first = firsts[group[0]]
        query_out, q_send = query_sum(q_own, back, q_outs, size, heads, first)
        q_outs = (query_out,)
        for rel in range(1, size):
            q_blocks.append(shifted(q_send[rel - 1][None], "head", -rel))
            q_plan.append((rel, first, (0,)))

    last = size - 1
    key_out, value_out = place(kv_blocks, tuple(kv_plan), kv_outs, size, heads)
    (query_out,) = place(q_blocks[:-last], tuple(q_plan[:-last]), q_outs, size, heads)
    (query_out,) = place(
        q_blocks[-last:], tuple(q_plan[-last:]), (query_out,), size, heads
    )
    return query_out[None], key_out[None], value_out[None]


def solution(mesh):
    in_specs = (
        P("group", None, "head"),
        P("group", None, "head"),
        P("group", None, "head"),
        P("group", None, "head"),
        P("group", "head", None),
        P("group", "head", None),
        P(),
        P(),
    )
    out_specs = (P("group", "head", None), P("group", "head", None), P("group", "head", None))

    return jax.shard_map(
        on_device, mesh=mesh, in_specs=in_specs, out_specs=out_specs, check_vma=False
    )
```

```python
import functools
import math

import jax
import jax.numpy as jnp
from jax import lax
from jax.experimental import pallas as pl
from jax.experimental.pallas import tpu as pltpu
from jax.sharding import PartitionSpec as P


HEAD_DIM = 128
STAT_ROWS = 24
DEAD = 1e30
LOG2E = 1.4426950408889634
VMEM_LIMIT = 30 * 1024 * 1024
KEY_TILE = 512
CHUNKS = (4, 4, 4, 4, 4)
MOVES = ((0,),)
GROUPS = ((0, 1), (2, 3, 4))


def shifted(block, axis, distance):
    size = lax.axis_size(axis)
    return lax.ppermute(block, axis, [(i, (i + distance) % size) for i in range(size)])


def passed_along(block, axis, distance):
    devices = range(lax.axis_size(axis))
    route = [(i - distance, i) for i in devices if i - distance in devices]
    return lax.ppermute(block, axis, route)


def chunks_of(head_count):
    if head_count == sum(CHUNKS):
        return CHUNKS
    count = min(head_count, len(CHUNKS))
    return tuple((head_count * (i + 1)) // count - (head_count * i) // count for i in range(count))


def within(groups, chunks):
    groups = [tuple(i for i in group if i < chunks) for group in groups]
    return [group for group in groups if group]


def three_parts(x):
    high = x.astype(jnp.bfloat16)
    rest = x - high.astype(jnp.float32)
    mid = rest.astype(jnp.bfloat16)
    low = (rest - mid.astype(jnp.float32)).astype(jnp.bfloat16)
    return high, mid, low


def cut_kernel(grad, *refs, plan, heads):
    outs, sems = refs[:-1], refs[-1]
    size = grad.shape[1] // (heads * HEAD_DIM)
    copies = []
    for i, (out, (rel, first)) in enumerate(zip(outs, plan)):
        peer = lax.rem(lax.axis_index("head") + rel, size)
        column = pl.multiple_of((peer * heads + first) * HEAD_DIM, HEAD_DIM)
        copies.append(
            pltpu.make_async_copy(grad.at[:, pl.ds(column, out.shape[1])], out, sems.at[i])
        )
    for copy in copies:
        copy.start()
    for copy in copies:
        copy.wait()


def cut(grad, heads, plan, counts):
    shapes = [(grad.shape[0], count * HEAD_DIM) for count in counts]
    return pl.pallas_call(
        functools.partial(cut_kernel, plan=plan, heads=heads),
        grid=(1,),
        in_specs=[pl.BlockSpec(memory_space=pl.ANY)],
        out_specs=[pl.BlockSpec(shape, lambda i: (0, 0)) for shape in shapes],
        out_shape=[jax.ShapeDtypeStruct(shape, jnp.bfloat16) for shape in shapes],
        scratch_shapes=[pltpu.SemaphoreType.DMA((len(plan),))],
        compiler_params=pltpu.CompilerParams(vmem_limit_bytes=VMEM_LIMIT),
        cost_estimate=pl.CostEstimate(
            flops=0,
            bytes_accessed=sum(4 * math.prod(shape) for shape in shapes),
            transcendentals=0,
        ),
        name="cut",
    )(grad)


def pack_kernel(grad, grad_recv, out, lse, *refs, first, joined):
    me = lax.axis_index("head")
    query, packed, scratch, sems = refs[0], refs[joined], refs[joined + 1 : -1], refs[-1]
    grad_own, out_own = scratch[:2]
    count, height, _ = packed.shape
    rows = out.shape[0]
    top = height - rows - STAT_ROWS
    per = grad.shape[0]
    size = rows // per
    lanes = rows // HEAD_DIM
    width = count * HEAD_DIM
    heads = out.shape[1] // HEAD_DIM
    column = pl.multiple_of((me * heads + first) * HEAD_DIM, HEAD_DIM)
    copies = [
        pltpu.make_async_copy(grad.at[:, pl.ds(column, width)], grad_own, sems.at[0]),
        pltpu.make_async_copy(out.at[:, pl.ds(first * HEAD_DIM, width)], out_own, sems.at[1]),
    ]
    if top:
        copies.append(
            pltpu.make_async_copy(
                query.at[:, pl.ds(first * HEAD_DIM, width)], scratch[2], sems.at[2]
            )
        )
    for copy in copies:
        copy.start()
    for copy in copies:
        copy.wait()
    ones = jnp.ones((16, HEAD_DIM), jnp.bfloat16)
    for h in range(count):
        cols = slice(h * HEAD_DIM, (h + 1) * HEAD_DIM)
        for r in range(size):
            start = pl.multiple_of(lax.rem(me - r + size, size) * per, per)
            block = grad_own[:, cols] if r == 0 else grad_recv[r - 1, :, cols]
            packed[h, pl.ds(pl.multiple_of(top + start, per), per), :] = block
        if top:
            packed[h, :top, :] = scratch[2][:, cols]
        product = packed[h, top : top + rows].astype(jnp.float32) * out_own[:, cols].astype(jnp.float32)
        delta = sum(
            lax.dot_general(
                ones, part, (((1,), (1,)), ((), ())), preferred_element_type=jnp.float32
            )
            for part in three_parts(product)
        )[:1]
        log_sum = lse[first + h] * LOG2E
        parts = three_parts(delta) + three_parts(log_sum)
        pieces = [
            part[:, j * HEAD_DIM : (j + 1) * HEAD_DIM].astype(jnp.float32)
            for part in parts
            for j in range(lanes)
        ]
        if len(pieces) < STAT_ROWS:
            pieces.append(jnp.zeros((STAT_ROWS - len(pieces), HEAD_DIM), jnp.float32))
        packed[h, top + rows :, :] = jnp.concatenate(pieces, axis=0).astype(jnp.bfloat16)


def pack(grad, grad_recv, out, lse, query, first, count, joined):
    rows = out.shape[0]
    per = grad.shape[0]
    height = rows * (1 + joined) + STAT_ROWS
    width = count * HEAD_DIM
    any_spec = pl.BlockSpec(memory_space=pltpu.HBM if first == 0 else pl.ANY)
    return pl.pallas_call(
        functools.partial(pack_kernel, first=first, joined=joined),
        grid_spec=pltpu.PrefetchScalarGridSpec(
            num_scalar_prefetch=0,
            grid=(1,),
            in_specs=[
                any_spec,
                pl.BlockSpec(grad_recv.shape, lambda i: (0, 0, 0)),
                any_spec,
                pl.BlockSpec(lse.shape, lambda i: (0, 0, 0)),
            ]
            + [any_spec] * joined,
            out_specs=pl.BlockSpec((count, height, HEAD_DIM), lambda i: (0, 0, 0)),
            scratch_shapes=[
                pltpu.VMEM((per, width), jnp.bfloat16),
                pltpu.VMEM((rows, width), jnp.bfloat16),
            ]
            + [pltpu.VMEM((rows, width), jnp.bfloat16)] * joined
            + [pltpu.SemaphoreType.DMA((2 + joined,))],
        ),
        out_shape=jax.ShapeDtypeStruct((count, height, HEAD_DIM), jnp.bfloat16),
        compiler_params=pltpu.CompilerParams(vmem_limit_bytes=VMEM_LIMIT),
        cost_estimate=pl.CostEstimate(
            flops=count * rows * HEAD_DIM * 16,
            bytes_accessed=count * rows * HEAD_DIM * 6,
            transcendentals=0,
        ),
        name="pack",
    )(grad, grad_recv, out, lse, *[query] * joined)


def stat_row(stats, at, lanes):
    total = (
        stats[at : at + lanes] + stats[at + lanes : at + 2 * lanes]
    ) + stats[at + 2 * lanes : at + 3 * lanes]
    return jnp.concatenate([total[j : j + 1] for j in range(lanes)], axis=1)


def stat_rows(packed, at, rows, query_len):
    lanes = rows // HEAD_DIM
    stats = packed[at, packed.shape[1] - STAT_ROWS :, :].astype(jnp.float32)
    alive = lax.broadcasted_iota(jnp.int32, (1, rows), 1) < query_len
    log_sum = jnp.where(alive, stat_row(stats, 3 * lanes, lanes), DEAD)
    return stat_row(stats, 0, lanes), log_sum


def head_grads(key, value, queries, grad, stats, own_len, both, tile):
    rows = key.shape[0]
    scale = HEAD_DIM**-0.5
    across = (((1,), (1,)), ((), ()))
    live_t = lax.broadcasted_iota(jnp.int32, (1, rows), 1) < own_len
    key_t = jnp.where(live_t, key[...].astype(jnp.float32).T, 0.0).astype(jnp.bfloat16)
    all_queries, all_grad = jnp.concatenate(queries, axis=0), jnp.concatenate(grad, axis=0)
    dq_t = None
    for at in range(0, rows, tile):
        k, v = key[at : at + tile, :], value[at : at + tile, :]
        probs, grad_scores = [], []
        for i, (delta, log_sum) in enumerate(stats):
            scores = lax.dot_general(k, queries[i], across, preferred_element_type=jnp.float32)
            prob = jnp.exp2(scores * (scale * LOG2E) - log_sum)
            grad_prob = lax.dot_general(v, grad[i], across, preferred_element_type=jnp.float32)
            grad_scores.append((prob * (grad_prob - delta)).astype(jnp.bfloat16))
            probs.append(prob.astype(jnp.bfloat16))
        probs = jnp.concatenate(probs, axis=1)
        grad_scores = jnp.concatenate(grad_scores, axis=1)
        dv = jnp.dot(probs, all_grad, preferred_element_type=jnp.float32)
        dk = jnp.dot(grad_scores, all_queries, preferred_element_type=jnp.float32)
        live = lax.broadcasted_iota(jnp.int32, (tile, 1), 0) + at < own_len
        both[0, at : at + tile, :] = jnp.where(live, dk * scale, 0.0).astype(jnp.bfloat16)
        both[1, at : at + tile, :] = jnp.where(live, dv, 0.0).astype(jnp.bfloat16)
        part = jnp.dot(
            key_t[:, at : at + tile], grad_scores, preferred_element_type=jnp.float32
        )
        dq_t = part if dq_t is None else dq_t + part
    return dq_t


def grads_kernel(lengths, sources, *refs, carried, tile):
    key, value, query, own, next_query, following = refs[:6]
    refs = refs[6 + carried :]
    key_out, value_out, send, query_own, query_cross, both = refs
    me, group_at = lax.axis_index("head"), lax.axis_index("group")
    own_len = lengths[group_at]
    after = lax.min(group_at + 1, lengths.shape[0] - 1)
    linked = (group_at + 1 == after) & (sources[after] == group_at)
    cross_len = jnp.where(linked, lengths[after], 0)
    rows = key.shape[0]
    per = key_out.shape[0]
    size = rows // per
    for p in range(query_own.shape[0]):
        cols = slice(p * HEAD_DIM, (p + 1) * HEAD_DIM)
        top = own.shape[1] - rows - STAT_ROWS
        queries = (query[:, cols], following[p, :rows, :] if top else next_query[:, cols])
        stats = (stat_rows(own, p, rows, own_len), stat_rows(following, p, rows, cross_len))
        grad = (own[p, top : top + rows, :], following[p, top : top + rows, :])
        dq_t = head_grads(
            key.at[:, cols], value.at[:, cols], queries, grad, stats, own_len, both.at[:, :, cols], tile
        )
        query_own[p] = dq_t[:, :rows].T * HEAD_DIM**-0.5
        query_cross[p] = (dq_t[:, rows:].T * HEAD_DIM**-0.5).astype(jnp.bfloat16)
    for r in range(size):
        start = pl.multiple_of(lax.rem(me - r + size, size) * per, per)
        if r == 0:
            key_out[...] = both[0, pl.ds(start, per), :]
            value_out[...] = both[1, pl.ds(start, per), :]
        else:
            send[r - 1, 0] = both[0, pl.ds(start, per), :]
            send[r - 1, 1] = both[1, pl.ds(start, per), :]


def grads(
    lengths, sources, key, value, query, own, next_query, next_first, following, carried, aliases,
    size, first, count, base, total,
):
    rows, width = key.shape
    per = rows // size
    heads = width // HEAD_DIM
    step = 2 if not any(n % 2 for n in (heads, first, count, base, next_first)) else 1
    wide = step * HEAD_DIM
    height = own.shape[1]
    any_spec = pl.BlockSpec(memory_space=pl.ANY)
    own_spec = pl.BlockSpec(
        (per, wide), lambda h, *_: (0, (lax.axis_index("head") * heads + first) // step + h)
    )
    full = jax.ShapeDtypeStruct((per, width * size), jnp.bfloat16)
    return pl.pallas_call(
        functools.partial(grads_kernel, carried=len(carried), tile=min(KEY_TILE, rows)),
        grid_spec=pltpu.PrefetchScalarGridSpec(
            num_scalar_prefetch=2,
            grid=(count // step,),
            in_specs=[
                pl.BlockSpec((rows, wide), lambda h, *_: (0, first // step + h)),
                pl.BlockSpec((rows, wide), lambda h, *_: (0, first // step + h)),
                pl.BlockSpec((rows, wide), lambda h, *_: (0, first // step + h)),
                pl.BlockSpec((step, height, HEAD_DIM), lambda h, *_: (h, 0, 0)),
                pl.BlockSpec((rows, wide), lambda h, *_: (0, (first - next_first) // step + h))
                if height == rows + STAT_ROWS
                else any_spec,
                pl.BlockSpec((step, height, HEAD_DIM), lambda h, *_: (h, 0, 0)),
            ]
            + [any_spec] * len(carried),
            out_specs=[
                own_spec,
                own_spec,
                pl.BlockSpec((size - 1, 2, per, wide), lambda h, *_: (0, 0, 0, h)),
                pl.BlockSpec((step, rows, HEAD_DIM), lambda h, *_: (base // step + h, 0, 0)),
                pl.BlockSpec((step, rows, HEAD_DIM), lambda h, *_: (base // step + h, 0, 0)),
            ],
            scratch_shapes=[pltpu.VMEM((2, rows, wide), jnp.bfloat16)],
        ),
        out_shape=[
            full,
            full,
            jax.ShapeDtypeStruct((size - 1, 2, per, count * HEAD_DIM), jnp.bfloat16),
            jax.ShapeDtypeStruct((total, rows, HEAD_DIM), jnp.float32),
            jax.ShapeDtypeStruct((total, rows, HEAD_DIM), jnp.bfloat16),
        ],
        input_output_aliases={8 + i: out for i, out in enumerate(aliases)},
        compiler_params=pltpu.CompilerParams(vmem_limit_bytes=VMEM_LIMIT),
        cost_estimate=pl.CostEstimate(
            flops=count * 20 * rows * rows * HEAD_DIM,
            bytes_accessed=count * rows * HEAD_DIM * 24,
            transcendentals=count * 2 * rows * rows,
        ),
        name="grads",
    )(lengths, sources, key, value, query, own, next_query, following, *carried)


def query_kernel(own, back, *refs, carried, first, heads):
    query_out, send, total, sem = refs[carried:]
    me = lax.axis_index("head")
    count, rows, _ = own.shape
    per = query_out.shape[0]
    size = rows // per
    for h in range(count):
        cols = slice(h * HEAD_DIM, (h + 1) * HEAD_DIM)
        total[:, cols] = (own[h] + back[h].astype(jnp.float32)).astype(jnp.bfloat16)
    column = pl.multiple_of((me * heads + first) * HEAD_DIM, HEAD_DIM)
    start = pl.multiple_of(me * per, per)
    copy = pltpu.make_async_copy(
        total.at[pl.ds(start, per), :],
        query_out.at[:, pl.ds(column, count * HEAD_DIM)],
        sem.at[0],
    )
    copy.start()
    for r in range(1, size):
        start = pl.multiple_of(lax.rem(me - r + size, size) * per, per)
        send[r - 1] = total[pl.ds(start, per), :]
    copy.wait()


def query_sum(own, back, carried, size, heads, first):
    count, rows, _ = own.shape
    per = rows // size
    any_spec = pl.BlockSpec(memory_space=pl.ANY)
    whole = (count, rows, HEAD_DIM)
    return pl.pallas_call(
        functools.partial(query_kernel, carried=len(carried), first=first, heads=heads),
        grid_spec=pltpu.PrefetchScalarGridSpec(
            num_scalar_prefetch=0,
            grid=(1,),
            in_specs=[
                pl.BlockSpec(whole, lambda i: (0, 0, 0)),
                pl.BlockSpec(whole, lambda i: (0, 0, 0)),
            ]
            + [any_spec] * len(carried),
            out_specs=[
                any_spec,
                pl.BlockSpec((size - 1, per, count * HEAD_DIM), lambda i: (0, 0, 0)),
            ],
            scratch_shapes=[
                pltpu.VMEM((rows, count * HEAD_DIM), jnp.bfloat16),
                pltpu.SemaphoreType.DMA((1,)),
            ],
        ),
        out_shape=[
            jax.ShapeDtypeStruct((per, heads * size * HEAD_DIM), jnp.bfloat16),
            jax.ShapeDtypeStruct((size - 1, per, count * HEAD_DIM), jnp.bfloat16),
        ],
        input_output_aliases={2 + i: i for i in range(len(carried))},
        compiler_params=pltpu.CompilerParams(vmem_limit_bytes=VMEM_LIMIT),
        cost_estimate=pl.CostEstimate(
            flops=count * rows * HEAD_DIM,
            bytes_accessed=count * rows * HEAD_DIM * 8,
            transcendentals=0,
        ),
        name="query_sum",
    )(own, back, *carried)


def place_kernel(*refs, plan, targets, size, heads):
    blocks = refs[: len(plan)]
    outs = refs[len(plan) + targets : len(plan) + 2 * targets]
    sems = refs[-1]
    me = lax.axis_index("head")
    copies = []
    for block, (rel, first, dests) in zip(blocks, plan):
        peer = lax.rem(me + rel, size)
        width = block.shape[-1]
        column = pl.multiple_of((peer * heads + first) * HEAD_DIM, HEAD_DIM)
        for j, dest in enumerate(dests):
            copies.append(
                pltpu.make_async_copy(
                    block.at[j], outs[dest].at[:, pl.ds(column, width)], sems.at[len(copies)]
                )
            )
    for copy in copies:
        copy.start()
    for copy in copies:
        copy.wait()


def place(blocks, plan, outs, size, heads):
    any_spec = pl.BlockSpec(memory_space=pl.ANY)
    copies = sum(len(dests) for _, _, dests in plan)
    return pl.pallas_call(
        functools.partial(
            place_kernel, plan=plan, targets=len(outs), size=size, heads=heads
        ),
        grid_spec=pltpu.PrefetchScalarGridSpec(
            num_scalar_prefetch=0,
            grid=(1,),
            in_specs=[
                any_spec
                for _ in (*blocks, *outs)
            ],
            out_specs=[any_spec] * len(outs),
            scratch_shapes=[pltpu.SemaphoreType.DMA((copies,))],
        ),
        out_shape=[jax.ShapeDtypeStruct(o.shape, o.dtype) for o in outs],
        input_output_aliases={len(blocks) + i: i for i in range(len(outs))},
        compiler_params=pltpu.CompilerParams(vmem_limit_bytes=VMEM_LIMIT),
        cost_estimate=pl.CostEstimate(
            flops=0,
            bytes_accessed=sum(4 * math.prod(b.shape) for b in blocks),
            transcendentals=0,
        ),
        name="place",
    )(*blocks, *outs)


def on_device(query, key, value, output, grad_out, log_sum, group_length, cache_source):
    size = lax.axis_size("head")
    me = lax.axis_index("head")
    query, key, value, output = query[0], key[0], value[0], output[0]
    grad, lse = grad_out[0], log_sum[0][:, None, :]
    width = query.shape[1]
    heads = width // HEAD_DIM
    counts = chunks_of(heads)
    firsts = [sum(counts[:i]) for i in range(len(counts))]

    rels = range(1, size)
    moves = within(MOVES, len(counts))
    plan = [(rel, firsts[i]) for i in range(1, len(counts)) for rel in rels]
    widths = [counts[i] for i in range(1, len(counts)) for rel in rels]
    pieces = cut(grad, heads, tuple(plan), widths)
    pieces = list(pieces)
    for rel in reversed(rels):
        start = (lax.rem(me + rel, size) * heads + firsts[0]) * HEAD_DIM
        block = lax.dynamic_slice_in_dim(grad, start, counts[0] * HEAD_DIM, axis=1)
        pieces = [block] + pieces

    received = []
    for i in range(len(counts)):
        blocks = []
        for rel in rels:
            blocks.append(shifted(pieces[i * (size - 1) + rel - 1], "head", rel)[None])
        received.append(blocks[0] if size == 2 else jnp.concatenate(blocks, axis=0))

    next_queries = {}
    for group in moves:
        start, end = firsts[group[0]], firsts[group[-1]] + counts[group[-1]]
        block = query[:, start * HEAD_DIM : end * HEAD_DIM]
        moved = passed_along(block, "group", -1)
        for i in group:
            next_queries[i] = (moved, firsts[group[0]])

    packs, nexts = [], []
    for i, (first, count) in enumerate(zip(firsts, counts)):
        joined = int(i not in next_queries)
        packs.append(pack(grad, received[i], output, lse, query, first, count, joined))
        nexts.append(passed_along(packs[i], "group", -1))

    kv_outs, q_outs = (), ()
    kv_blocks, kv_plan, q_blocks, q_plan = [], [], [], []
    for group in within(GROUPS, len(counts)):
        total = sum(counts[i] for i in group)
        base, q_parts = 0, ()
        for i in group:
            aliases = ((0, 1) if kv_outs else ()) + ((3, 4) if q_parts else ())
            key_out, value_out, kv_send, q_own, q_cross = grads(
                group_length, cache_source, key, value, query, packs[i], *next_queries.get(i, (query, 0)), nexts[i],
                kv_outs + q_parts, aliases, size, firsts[i], counts[i], base, total,
            )
            kv_outs, q_parts = (key_out, value_out), (q_own, q_cross)
            base += counts[i]
            for rel in range(1, size):
                kv_blocks.append(shifted(kv_send[rel - 1], "head", -rel))
                kv_plan.append((rel, firsts[i], (0, 1)))
        back = passed_along(q_cross, "group", 1)
        first = firsts[group[0]]
        query_out, q_send = query_sum(q_own, back, q_outs, size, heads, first)
        q_outs = (query_out,)
        for rel in range(1, size):
            q_blocks.append(shifted(q_send[rel - 1][None], "head", -rel))
            q_plan.append((rel, first, (0,)))

    last = size - 1
    key_out, value_out = place(kv_blocks, tuple(kv_plan), kv_outs, size, heads)
    (query_out,) = place(q_blocks[:-last], tuple(q_plan[:-last]), q_outs, size, heads)
    (query_out,) = place(
        q_blocks[-last:], tuple(q_plan[-last:]), (query_out,), size, heads
    )
    return query_out[None], key_out[None], value_out[None]


def solution(mesh):
    in_specs = (
        P("group", None, "head"),
        P("group", None, "head"),
        P("group", None, "head"),
        P("group", None, "head"),
        P("group", "head", None),
        P("group", "head", None),
        P(),
        P(),
    )
    out_specs = (P("group", "head", None), P("group", "head", None), P("group", "head", None))

    return jax.shard_map(
        on_device, mesh=mesh, in_specs=in_specs, out_specs=out_specs, check_vma=False
    )
```

```python
import functools
import math

import jax
import jax.numpy as jnp
from jax import lax
from jax.experimental import pallas as pl
from jax.experimental.pallas import tpu as pltpu
from jax.sharding import PartitionSpec as P


HEAD_DIM = 128
STAT_ROWS = 32
DEAD = 1e30
LOG2E = 1.4426950408889634
VMEM_LIMIT = 24 * 1024 * 1024
KEY_TILE = 512
CHUNKS = (4, 4, 4, 4, 4)
MOVES = ((0,),)
GROUPS = ((0, 1, 2), (3, 4))


def shifted(block, axis, distance):
    size = lax.axis_size(axis)
    return lax.ppermute(block, axis, [(i, (i + distance) % size) for i in range(size)])


def passed_along(block, axis, distance):
    devices = range(lax.axis_size(axis))
    route = [(i - distance, i) for i in devices if i - distance in devices]
    return lax.ppermute(block, axis, route)


def chunks_of(head_count):
    if head_count == sum(CHUNKS):
        return CHUNKS
    count = min(head_count, len(CHUNKS))
    return tuple((head_count * (i + 1)) // count - (head_count * i) // count for i in range(count))


def within(groups, chunks):
    groups = [tuple(i for i in group if i < chunks) for group in groups]
    return [group for group in groups if group]


def three_parts(x):
    high = x.astype(jnp.bfloat16)
    rest = x - high.astype(jnp.float32)
    mid = rest.astype(jnp.bfloat16)
    low = (rest - mid.astype(jnp.float32)).astype(jnp.bfloat16)
    return high, mid, low


def cut_kernel(grad, *refs, plan, heads):
    outs, sems = refs[:-1], refs[-1]
    size = grad.shape[1] // (heads * HEAD_DIM)
    copies = []
    for i, (out, (rel, first)) in enumerate(zip(outs, plan)):
        peer = lax.rem(lax.axis_index("head") + rel, size)
        column = pl.multiple_of((peer * heads + first) * HEAD_DIM, HEAD_DIM)
        copies.append(
            pltpu.make_async_copy(grad.at[:, pl.ds(column, out.shape[1])], out, sems.at[i])
        )
    for copy in copies:
        copy.start()
    for copy in copies:
        copy.wait()


def cut(grad, heads, plan, counts):
    shapes = [(grad.shape[0], count * HEAD_DIM) for count in counts]
    return pl.pallas_call(
        functools.partial(cut_kernel, plan=plan, heads=heads),
        grid=(1,),
        in_specs=[pl.BlockSpec(memory_space=pl.ANY)],
        out_specs=[pl.BlockSpec(shape, lambda i: (0, 0)) for shape in shapes],
        out_shape=[jax.ShapeDtypeStruct(shape, jnp.bfloat16) for shape in shapes],
        scratch_shapes=[pltpu.SemaphoreType.DMA((len(plan),))],
        compiler_params=pltpu.CompilerParams(vmem_limit_bytes=VMEM_LIMIT),
        cost_estimate=pl.CostEstimate(
            flops=0,
            bytes_accessed=sum(4 * math.prod(shape) for shape in shapes),
            transcendentals=0,
        ),
        name="cut",
    )(grad)


def pack_kernel(grad, grad_recv, out, lse, *refs, first, joined):
    me = lax.axis_index("head")
    query, packed, scratch, sems = refs[0], refs[joined], refs[joined + 1 : -1], refs[-1]
    grad_own, out_own = scratch[:2]
    count, height, _ = packed.shape
    rows = out.shape[0]
    top = height - rows - STAT_ROWS
    per = grad.shape[0]
    size = rows // per
    lanes = rows // HEAD_DIM
    width = count * HEAD_DIM
    heads = out.shape[1] // HEAD_DIM
    column = pl.multiple_of((me * heads + first) * HEAD_DIM, HEAD_DIM)
    copies = [
        pltpu.make_async_copy(grad.at[:, pl.ds(column, width)], grad_own, sems.at[0]),
        pltpu.make_async_copy(out.at[:, pl.ds(first * HEAD_DIM, width)], out_own, sems.at[1]),
    ]
    if top:
        copies.append(
            pltpu.make_async_copy(
                query.at[:, pl.ds(first * HEAD_DIM, width)], scratch[2], sems.at[2]
            )
        )
    for copy in copies:
        copy.start()
    for copy in copies:
        copy.wait()
    ones = jnp.ones((16, HEAD_DIM), jnp.bfloat16)
    for h in range(count):
        cols = slice(h * HEAD_DIM, (h + 1) * HEAD_DIM)
        for r in range(size):
            start = pl.multiple_of(lax.rem(me - r + size, size) * per, per)
            block = grad_own[:, cols] if r == 0 else grad_recv[r - 1, :, cols]
            packed[h, pl.ds(pl.multiple_of(top + start, per), per), :] = block
        if top:
            packed[h, :top, :] = scratch[2][:, cols]
        product = packed[h, top : top + rows].astype(jnp.float32) * out_own[:, cols].astype(jnp.float32)
        delta = sum(
            lax.dot_general(
                ones, part, (((1,), (1,)), ((), ())), preferred_element_type=jnp.float32
            )
            for part in three_parts(product)
        )[:1]
        log_sum = lse[first + h] * LOG2E
        parts = three_parts(delta) + three_parts(log_sum)
        pieces = [
            part[:, j * HEAD_DIM : (j + 1) * HEAD_DIM].astype(jnp.float32)
            for part in parts
            for j in range(lanes)
        ]
        pieces.append(jnp.zeros((STAT_ROWS - len(pieces), HEAD_DIM), jnp.float32))
        packed[h, top + rows :, :] = jnp.concatenate(pieces, axis=0).astype(jnp.bfloat16)


def pack(grad, grad_recv, out, lse, query, first, count, joined):
    rows = out.shape[0]
    per = grad.shape[0]
    height = rows * (1 + joined) + STAT_ROWS
    width = count * HEAD_DIM
    any_spec = pl.BlockSpec(memory_space=pltpu.HBM if first == 0 else pl.ANY)
    return pl.pallas_call(
        functools.partial(pack_kernel, first=first, joined=joined),
        grid_spec=pltpu.PrefetchScalarGridSpec(
            num_scalar_prefetch=0,
            grid=(1,),
            in_specs=[
                any_spec,
                pl.BlockSpec(grad_recv.shape, lambda i: (0, 0, 0)),
                any_spec,
                pl.BlockSpec(lse.shape, lambda i: (0, 0, 0)),
            ]
            + [any_spec] * joined,
            out_specs=pl.BlockSpec((count, height, HEAD_DIM), lambda i: (0, 0, 0)),
            scratch_shapes=[
                pltpu.VMEM((per, width), jnp.bfloat16),
                pltpu.VMEM((rows, width), jnp.bfloat16),
            ]
            + [pltpu.VMEM((rows, width), jnp.bfloat16)] * joined
            + [pltpu.SemaphoreType.DMA((2 + joined,))],
        ),
        out_shape=jax.ShapeDtypeStruct((count, height, HEAD_DIM), jnp.bfloat16),
        compiler_params=pltpu.CompilerParams(vmem_limit_bytes=VMEM_LIMIT),
        cost_estimate=pl.CostEstimate(
            flops=count * rows * HEAD_DIM * 16,
            bytes_accessed=count * rows * HEAD_DIM * 6,
            transcendentals=0,
        ),
        name="pack",
    )(grad, grad_recv, out, lse, *[query] * joined)


def stat_row(stats, at, lanes):
    total = (
        stats[at : at + lanes] + stats[at + lanes : at + 2 * lanes]
    ) + stats[at + 2 * lanes : at + 3 * lanes]
    return jnp.concatenate([total[j : j + 1] for j in range(lanes)], axis=1)


def stat_rows(packed, at, rows, query_len):
    lanes = rows // HEAD_DIM
    stats = packed[at, packed.shape[1] - STAT_ROWS :, :].astype(jnp.float32)
    alive = lax.broadcasted_iota(jnp.int32, (1, rows), 1) < query_len
    log_sum = jnp.where(alive, stat_row(stats, 3 * lanes, lanes), DEAD)
    return stat_row(stats, 0, lanes), log_sum


def head_grads(key, value, queries, grad, stats, own_len, both, tile):
    rows = key.shape[0]
    scale = HEAD_DIM**-0.5
    across = (((1,), (1,)), ((), ()))
    live_t = lax.broadcasted_iota(jnp.int32, (1, rows), 1) < own_len
    key_t = jnp.where(live_t, key[...].astype(jnp.float32).T, 0.0).astype(jnp.bfloat16)
    all_queries, all_grad = jnp.concatenate(queries, axis=0), jnp.concatenate(grad, axis=0)
    dq_t = None
    for at in range(0, rows, tile):
        k, v = key[at : at + tile, :], value[at : at + tile, :]
        probs, grad_scores = [], []
        for i, (delta, log_sum) in enumerate(stats):
            scores = lax.dot_general(k, queries[i], across, preferred_element_type=jnp.float32)
            prob = jnp.exp2(scores * (scale * LOG2E) - log_sum)
            grad_prob = lax.dot_general(v, grad[i], across, preferred_element_type=jnp.float32)
            grad_scores.append((prob * (grad_prob - delta)).astype(jnp.bfloat16))
            probs.append(prob.astype(jnp.bfloat16))
        probs = jnp.concatenate(probs, axis=1)
        grad_scores = jnp.concatenate(grad_scores, axis=1)
        dv = jnp.dot(probs, all_grad, preferred_element_type=jnp.float32)
        dk = jnp.dot(grad_scores, all_queries, preferred_element_type=jnp.float32)
        live = lax.broadcasted_iota(jnp.int32, (tile, 1), 0) + at < own_len
        both[0, at : at + tile, :] = jnp.where(live, dk * scale, 0.0).astype(jnp.bfloat16)
        both[1, at : at + tile, :] = jnp.where(live, dv, 0.0).astype(jnp.bfloat16)
        part = jnp.dot(
            key_t[:, at : at + tile], grad_scores, preferred_element_type=jnp.float32
        )
        dq_t = part if dq_t is None else dq_t + part
    return dq_t


def grads_kernel(lengths, sources, *refs, carried, tile):
    key, value, query, own, next_query, following = refs[:6]
    refs = refs[6 + carried :]
    key_out, value_out, send, query_own, query_cross, both = refs
    me, group_at = lax.axis_index("head"), lax.axis_index("group")
    own_len = lengths[group_at]
    after = lax.min(group_at + 1, lengths.shape[0] - 1)
    linked = (group_at + 1 == after) & (sources[after] == group_at)
    cross_len = jnp.where(linked, lengths[after], 0)
    rows = key.shape[0]
    per = key_out.shape[0]
    size = rows // per
    for p in range(query_own.shape[0]):
        cols = slice(p * HEAD_DIM, (p + 1) * HEAD_DIM)
        top = own.shape[1] - rows - STAT_ROWS
        queries = (query[:, cols], following[p, :rows, :] if top else next_query[:, cols])
        stats = (stat_rows(own, p, rows, own_len), stat_rows(following, p, rows, cross_len))
        grad = (own[p, top : top + rows, :], following[p, top : top + rows, :])
        dq_t = head_grads(
            key.at[:, cols], value.at[:, cols], queries, grad, stats, own_len, both.at[:, :, cols], tile
        )
        query_own[p] = dq_t[:, :rows].T * HEAD_DIM**-0.5
        query_cross[p] = (dq_t[:, rows:].T * HEAD_DIM**-0.5).astype(jnp.bfloat16)
    for r in range(size):
        start = pl.multiple_of(lax.rem(me - r + size, size) * per, per)
        if r == 0:
            key_out[...] = both[0, pl.ds(start, per), :]
            value_out[...] = both[1, pl.ds(start, per), :]
        else:
            send[r - 1, 0] = both[0, pl.ds(start, per), :]
            send[r - 1, 1] = both[1, pl.ds(start, per), :]


def grads(
    lengths, sources, key, value, query, own, next_query, next_first, following, carried, aliases,
    size, first, count, base, total,
):
    rows, width = key.shape
    per = rows // size
    heads = width // HEAD_DIM
    step = 2 if not any(n % 2 for n in (heads, first, count, base, next_first)) else 1
    wide = step * HEAD_DIM
    height = own.shape[1]
    any_spec = pl.BlockSpec(memory_space=pl.ANY)
    own_spec = pl.BlockSpec(
        (per, wide), lambda h, *_: (0, (lax.axis_index("head") * heads + first) // step + h)
    )
    full = jax.ShapeDtypeStruct((per, width * size), jnp.bfloat16)
    return pl.pallas_call(
        functools.partial(grads_kernel, carried=len(carried), tile=min(KEY_TILE, rows)),
        grid_spec=pltpu.PrefetchScalarGridSpec(
            num_scalar_prefetch=2,
            grid=(count // step,),
            in_specs=[
                pl.BlockSpec((rows, wide), lambda h, *_: (0, first // step + h)),
                pl.BlockSpec((rows, wide), lambda h, *_: (0, first // step + h)),
                pl.BlockSpec((rows, wide), lambda h, *_: (0, first // step + h)),
                pl.BlockSpec((step, height, HEAD_DIM), lambda h, *_: (h, 0, 0)),
                pl.BlockSpec((rows, wide), lambda h, *_: (0, (first - next_first) // step + h))
                if height == rows + STAT_ROWS
                else any_spec,
                pl.BlockSpec((step, height, HEAD_DIM), lambda h, *_: (h, 0, 0)),
            ]
            + [any_spec] * len(carried),
            out_specs=[
                own_spec,
                own_spec,
                pl.BlockSpec((size - 1, 2, per, wide), lambda h, *_: (0, 0, 0, h)),
                pl.BlockSpec((step, rows, HEAD_DIM), lambda h, *_: (base // step + h, 0, 0)),
                pl.BlockSpec((step, rows, HEAD_DIM), lambda h, *_: (base // step + h, 0, 0)),
            ],
            scratch_shapes=[pltpu.VMEM((2, rows, wide), jnp.bfloat16)],
        ),
        out_shape=[
            full,
            full,
            jax.ShapeDtypeStruct((size - 1, 2, per, count * HEAD_DIM), jnp.bfloat16),
            jax.ShapeDtypeStruct((total, rows, HEAD_DIM), jnp.float32),
            jax.ShapeDtypeStruct((total, rows, HEAD_DIM), jnp.bfloat16),
        ],
        input_output_aliases={8 + i: out for i, out in enumerate(aliases)},
        compiler_params=pltpu.CompilerParams(vmem_limit_bytes=VMEM_LIMIT),
        cost_estimate=pl.CostEstimate(
            flops=count * 20 * rows * rows * HEAD_DIM,
            bytes_accessed=count * rows * HEAD_DIM * 24,
            transcendentals=count * 2 * rows * rows,
        ),
        name="grads",
    )(lengths, sources, key, value, query, own, next_query, following, *carried)


def query_kernel(own, back, *refs, carried, first, heads):
    query_out, send, total, sem = refs[carried:]
    me = lax.axis_index("head")
    count, rows, _ = own.shape
    per = query_out.shape[0]
    size = rows // per
    for h in range(count):
        cols = slice(h * HEAD_DIM, (h + 1) * HEAD_DIM)
        total[:, cols] = (own[h] + back[h].astype(jnp.float32)).astype(jnp.bfloat16)
    column = pl.multiple_of((me * heads + first) * HEAD_DIM, HEAD_DIM)
    start = pl.multiple_of(me * per, per)
    copy = pltpu.make_async_copy(
        total.at[pl.ds(start, per), :],
        query_out.at[:, pl.ds(column, count * HEAD_DIM)],
        sem.at[0],
    )
    copy.start()
    for r in range(1, size):
        start = pl.multiple_of(lax.rem(me - r + size, size) * per, per)
        send[r - 1] = total[pl.ds(start, per), :]
    copy.wait()


def query_sum(own, back, carried, size, heads, first):
    count, rows, _ = own.shape
    per = rows // size
    any_spec = pl.BlockSpec(memory_space=pl.ANY)
    whole = (count, rows, HEAD_DIM)
    return pl.pallas_call(
        functools.partial(query_kernel, carried=len(carried), first=first, heads=heads),
        grid_spec=pltpu.PrefetchScalarGridSpec(
            num_scalar_prefetch=0,
            grid=(1,),
            in_specs=[
                pl.BlockSpec(whole, lambda i: (0, 0, 0)),
                pl.BlockSpec(whole, lambda i: (0, 0, 0)),
            ]
            + [any_spec] * len(carried),
            out_specs=[
                any_spec,
                pl.BlockSpec((size - 1, per, count * HEAD_DIM), lambda i: (0, 0, 0)),
            ],
            scratch_shapes=[
                pltpu.VMEM((rows, count * HEAD_DIM), jnp.bfloat16),
                pltpu.SemaphoreType.DMA((1,)),
            ],
        ),
        out_shape=[
            jax.ShapeDtypeStruct((per, heads * size * HEAD_DIM), jnp.bfloat16),
            jax.ShapeDtypeStruct((size - 1, per, count * HEAD_DIM), jnp.bfloat16),
        ],
        input_output_aliases={2 + i: i for i in range(len(carried))},
        compiler_params=pltpu.CompilerParams(vmem_limit_bytes=VMEM_LIMIT),
        cost_estimate=pl.CostEstimate(
            flops=count * rows * HEAD_DIM,
            bytes_accessed=count * rows * HEAD_DIM * 8,
            transcendentals=0,
        ),
        name="query_sum",
    )(own, back, *carried)


def place_kernel(*refs, plan, targets, size, heads):
    blocks = refs[: len(plan)]
    outs = refs[len(plan) + targets : len(plan) + 2 * targets]
    sems = refs[-1]
    me = lax.axis_index("head")
    copies = []
    for block, (rel, first, dests) in zip(blocks, plan):
        peer = lax.rem(me + rel, size)
        width = block.shape[-1]
        column = pl.multiple_of((peer * heads + first) * HEAD_DIM, HEAD_DIM)
        for j, dest in enumerate(dests):
            copies.append(
                pltpu.make_async_copy(
                    block.at[j], outs[dest].at[:, pl.ds(column, width)], sems.at[len(copies)]
                )
            )
    for copy in copies:
        copy.start()
    for copy in copies:
        copy.wait()


def place(blocks, plan, outs, size, heads):
    any_spec = pl.BlockSpec(memory_space=pl.ANY)
    copies = sum(len(dests) for _, _, dests in plan)
    return pl.pallas_call(
        functools.partial(
            place_kernel, plan=plan, targets=len(outs), size=size, heads=heads
        ),
        grid_spec=pltpu.PrefetchScalarGridSpec(
            num_scalar_prefetch=0,
            grid=(1,),
            in_specs=[
                pl.BlockSpec(b.shape, functools.partial(lambda n, i: (0,) * n, b.ndim))
                for b in blocks
            ]
            + [any_spec] * len(outs),
            out_specs=[any_spec] * len(outs),
            scratch_shapes=[pltpu.SemaphoreType.DMA((copies,))],
        ),
        out_shape=[jax.ShapeDtypeStruct(o.shape, o.dtype) for o in outs],
        input_output_aliases={len(blocks) + i: i for i in range(len(outs))},
        compiler_params=pltpu.CompilerParams(vmem_limit_bytes=VMEM_LIMIT),
        cost_estimate=pl.CostEstimate(
            flops=0,
            bytes_accessed=sum(4 * math.prod(b.shape) for b in blocks),
            transcendentals=0,
        ),
        name="place",
    )(*blocks, *outs)


def on_device(query, key, value, output, grad_out, log_sum, group_length, cache_source):
    size = lax.axis_size("head")
    me = lax.axis_index("head")
    query, key, value, output = query[0], key[0], value[0], output[0]
    grad, lse = grad_out[0], log_sum[0][:, None, :]
    width = query.shape[1]
    heads = width // HEAD_DIM
    counts = chunks_of(heads)
    firsts = [sum(counts[:i]) for i in range(len(counts))]

    rels = range(1, size)
    moves = within(MOVES, len(counts))
    plan = [(rel, firsts[i]) for i in range(1, len(counts)) for rel in rels]
    widths = [counts[i] for i in range(1, len(counts)) for rel in rels]
    pieces = cut(grad, heads, tuple(plan), widths)
    pieces = list(pieces)
    for rel in reversed(rels):
        start = (lax.rem(me + rel, size) * heads + firsts[0]) * HEAD_DIM
        block = lax.dynamic_slice_in_dim(grad, start, counts[0] * HEAD_DIM, axis=1)
        pieces = [block] + pieces

    received = []
    for i in range(len(counts)):
        blocks = []
        for rel in rels:
            blocks.append(shifted(pieces[i * (size - 1) + rel - 1], "head", rel)[None])
        received.append(blocks[0] if size == 2 else jnp.concatenate(blocks, axis=0))

    next_queries = {}
    for group in moves:
        start, end = firsts[group[0]], firsts[group[-1]] + counts[group[-1]]
        block = query[:, start * HEAD_DIM : end * HEAD_DIM]
        moved = passed_along(block, "group", -1)
        for i in group:
            next_queries[i] = (moved, firsts[group[0]])

    packs, nexts = [], []
    for i, (first, count) in enumerate(zip(firsts, counts)):
        joined = int(i not in next_queries)
        packs.append(pack(grad, received[i], output, lse, query, first, count, joined))
        nexts.append(passed_along(packs[i], "group", -1))

    kv_outs, q_outs = (), ()
    kv_blocks, kv_plan, q_blocks, q_plan = [], [], [], []
    for group in within(GROUPS, len(counts)):
        total = sum(counts[i] for i in group)
        base, q_parts = 0, ()
        for i in group:
            aliases = ((0, 1) if kv_outs else ()) + ((3, 4) if q_parts else ())
            key_out, value_out, kv_send, q_own, q_cross = grads(
                group_length, cache_source, key, value, query, packs[i], *next_queries.get(i, (query, 0)), nexts[i],
                kv_outs + q_parts, aliases, size, firsts[i], counts[i], base, total,
            )
            kv_outs, q_parts = (key_out, value_out), (q_own, q_cross)
            base += counts[i]
            for rel in range(1, size):
                kv_blocks.append(shifted(kv_send[rel - 1], "head", -rel))
                kv_plan.append((rel, firsts[i], (0, 1)))
        back = passed_along(q_cross, "group", 1)
        first = firsts[group[0]]
        query_out, q_send = query_sum(q_own, back, q_outs, size, heads, first)
        q_outs = (query_out,)
        for rel in range(1, size):
            q_blocks.append(shifted(q_send[rel - 1][None], "head", -rel))
            q_plan.append((rel, first, (0,)))

    last = size - 1
    key_out, value_out = place(kv_blocks, tuple(kv_plan), kv_outs, size, heads)
    (query_out,) = place(q_blocks[:-last], tuple(q_plan[:-last]), q_outs, size, heads)
    (query_out,) = place(
        q_blocks[-last:], tuple(q_plan[-last:]), (query_out,), size, heads
    )
    return query_out[None], key_out[None], value_out[None]


def solution(mesh):
    in_specs = (
        P("group", None, "head"),
        P("group", None, "head"),
        P("group", None, "head"),
        P("group", None, "head"),
        P("group", "head", None),
        P("group", "head", None),
        P(),
        P(),
    )
    out_specs = (P("group", "head", None), P("group", "head", None), P("group", "head", None))

    return jax.shard_map(
        on_device, mesh=mesh, in_specs=in_specs, out_specs=out_specs, check_vma=False
    )
```
